32 devices in a mesh: ctx: 8 (over z, y), tp: 4 (over x, core).
Axes of the slice: x: 2, y: 2, z: 4, core: 2. Of those that a mesh axis runs over, the one named last changes fastest.
Arguments:
- tokens: bfloat16 [4096, 4096], P('ctx', 'tp'), may hold values from -6 to 6
- w_in: bfloat16 [4096, 3, 2048], P(None, None, 'tp'), may hold values from -0.09375 to 0.09375
- conv_taps: float32 [3, 3, 2048], P(None, None, 'tp'), may hold values from -3 to 3
- long_filter: bfloat16 [4096, 2048], P('ctx', 'tp'), may hold values from -0.25 to 0.25
- skip_gain: float32 [2048], P('tp'), may hold values from 0.5 to 1.5
- w_out: bfloat16 [2048, 4096], P('tp'), may hold values from -0.1875 to 0.1875
Outputs:
- mixed: bfloat16 [4096, 4096], P('ctx', 'tp')
The draws below stay inside these ranges and needn't reach their ends.
All inputs are finite; a program needn't handle non-finite values.
Results may differ from the reference program's by a relative error of at most 0.0095.
Values may be sent and summed in bfloat16 or wider, within the bound.
No kernel may reach another device: no remote copies, remote signals or barrier semaphores. Data moves between devices by JAX's collectives and lax.ppermute only.
A program may use at most 128 MiB of HBM per device.

```python
import jax
import jax.numpy as jnp
from jax import lax

D = 4096
C = 2048
SEQ = 4096
CL = 512
N_TP = 4


def raised(array, key, source, target, parts, factor):
    def block_of(axis_at):
        return (jnp.arange(array.shape[axis_at]) // (array.shape[axis_at] // parts)).reshape((-1,) + (1,) * (array.ndim - 1 - axis_at))

    near = jax.random.permutation(key, parts)[block_of(target)]
    second = (block_of(target) + parts // 2) % parts
    return jnp.where((block_of(source) == near) | (block_of(source) == second), factor * array, array)


def block_scale(key, dims, cuts, low, largest):
    loudness = 1.0
    for position, blocks in cuts:
        draws = jax.random.uniform(jax.random.fold_in(jax.random.fold_in(key, 6), position), (blocks,), jnp.float32, low / len(cuts), largest / len(cuts))
        loudness = loudness * jnp.repeat(jnp.exp(draws), dims[position] // blocks).reshape((-1,) + (1,) * (len(dims) - 1 - position))
    return loudness


def bell_draw(rng, dims, width, limit, shards=(), held_as=jnp.bfloat16):
    gain = block_scale(rng, dims, shards, -0.22, 0.18) if shards else 1.0
    result = jax.random.normal(rng, dims, jnp.float32) * width * gain
    return jnp.minimum(jnp.maximum(result, -limit), limit).astype(held_as)


def noise_with(stream_key, dims, deviation, most, cuts, heavy, kind=jnp.bfloat16):
    result = deviation * jax.random.normal(stream_key, dims, jnp.float32)
    if cuts:
        result = result * block_scale(stream_key, dims, cuts, -0.22, 0.18)
    return jnp.clip(raised(result, jax.random.fold_in(stream_key, 3), *heavy), -most, most).astype(kind)


def setup_inputs(seed: int = 0) -> dict:
    key_of = jax.random.split(jax.random.key(seed), 7)
    tokens = bell_draw(key_of[0], (SEQ, D), 1.0, 6.0, ((0, 8), (1, 4)))
    w_in = bell_draw(key_of[1], (D, 3, C), D ** -0.5, 0.09375, ((2, 4),))
    conv_taps = bell_draw(key_of[2], (3, 3, C), 0.6, 3.0, ((2, 4),), jnp.float32)
    long_filter = bell_draw(key_of[3], (SEQ, C), (SEQ ** -0.5), 0.25, ((0, 8), (1, 4)))
    skip_gain = jnp.clip(0.5 + 1.0 * jax.random.uniform(key_of[4], (C,), jnp.float32) ** block_scale(key_of[4], (C,), ((0, 4),), -0.2, 0.2), 0.5, 1.5)
    w_out = noise_with(key_of[5], (C, D), C ** -0.5, 0.1875, ((0, 4),), (0, 1, 4, 2.0))
    return dict(tokens=tokens, w_in=w_in, conv_taps=conv_taps, long_filter=long_filter, skip_gain=skip_gain, w_out=w_out)


def reference(tokens, w_in, conv_taps, long_filter, skip_gain, w_out):
    seq_len = tokens.shape[0]
    projected = jnp.dot(tokens, w_in.reshape(D, 3 * C), preferred_element_type=jnp.float32).astype(jnp.bfloat16)
    shifted = jnp.pad(projected.astype(jnp.float32), ((2, 0), (0, 0)))
    tap_flat = conv_taps.reshape(3, 3 * C)
    features = tap_flat[0] * shifted[2:] + tap_flat[1] * shifted[1:-1] + tap_flat[2] * shifted[:-2]
    query_feat = features[:, :C]
    key_feat = features[:, C:2 * C]
    val_feat = features[:, 2 * C:]
    product_kv = (key_feat * val_feat).astype(jnp.bfloat16)
    spectrum = jnp.fft.rfft(product_kv.astype(jnp.float32), n=2 * seq_len, axis=0) * jnp.fft.rfft(long_filter.astype(jnp.float32), n=2 * seq_len, axis=0)
    conv_out = jnp.fft.irfft(spectrum, n=2 * seq_len, axis=0)[:seq_len].astype(jnp.bfloat16)
    gated_rows = (query_feat * (conv_out.astype(jnp.float32) + skip_gain * product_kv.astype(jnp.float32))).astype(jnp.bfloat16)
    g_blocks = gated_rows.reshape(seq_len, N_TP, CL).transpose(1, 0, 2)
    w_blocks = w_out.reshape(N_TP, CL, D)

    def add_block(running, block_pair):
        partial_out = jnp.dot(block_pair[0], block_pair[1], preferred_element_type=jnp.float32).astype(jnp.bfloat16)
        partial_out = lax.optimization_barrier(partial_out)
        return running + partial_out.astype(jnp.float32), None

    running, unused = lax.scan(add_block, jnp.zeros((seq_len, D), jnp.float32), (g_blocks, w_blocks))
    return running.astype(jnp.bfloat16)
```

```python
import functools
import math

import jax
import jax.numpy as jnp
import numpy as np
from jax import lax
from jax.experimental import pallas as pl
from jax.experimental.pallas import tpu as pltpu
from jax.sharding import PartitionSpec as P

LANES = 128
HALO = 16
F32 = jnp.float32
BF16 = jnp.bfloat16


def split_table(table):
    high = table.astype(BF16)
    low = (table - high.astype(np.float64)).astype(BF16)
    return high, low


def tables(seq_len):
    rows = seq_len // LANES
    size = 2 * seq_len
    kept = -(-(rows + 1) // 8) * 8
    k = np.arange(kept)[:, None]
    valid = (k <= rows).astype(np.float64)
    a = np.arange(rows)[None, :]
    b = np.arange(LANES)[None, :]
    turn = 2.0 * np.pi / (2 * rows) * (k * a % (2 * rows))
    outer = np.concatenate([np.cos(turn) * valid, -np.sin(turn) * valid], axis=0)
    outer_high, outer_low = split_table(outer)
    outer_both = np.concatenate([outer_high, outer_low], axis=1)
    twist = 2.0 * np.pi / size * (k * b % size)
    twist_cos = np.cos(twist).astype(np.float32)
    twist_sin = np.sin(twist).astype(np.float32)
    m = np.arange(LANES)
    angle = 2.0 * np.pi / LANES * (m[:, None] * m[None, :] % LANES)
    cos, sin = np.cos(angle), np.sin(angle)
    ahead = np.concatenate([np.concatenate([cos, -sin], 1), np.concatenate([sin, cos], 1)], 0)
    back = np.concatenate([np.concatenate([cos, sin], 1), np.concatenate([-sin, cos], 1)], 0)
    weight = np.where((k == 0) | (k == rows), 1.0, 2.0) * valid / size
    closing = np.concatenate([np.cos(turn) * weight, -np.sin(turn) * weight], axis=0).T
    closing_high, closing_low = split_table(closing)
    closing_all = np.concatenate([closing_high, closing_low, closing_high], axis=1)
    return dict(
        outer=outer_both, twist_cos=twist_cos, twist_sin=twist_sin,
        ahead=np.stack(split_table(ahead)), back=np.stack(split_table(back)),
        closing=closing_all, kept=kept, rows=rows,
    )


def dot(a, b):
    return jnp.dot(a, b, preferred_element_type=F32)


def dot3(value, table_ref):
    high = value.astype(BF16)
    low = (value - high.astype(F32)).astype(BF16)
    return dot(high, table_ref[0]) + dot(low, table_ref[0]) + dot(high, table_ref[1])


def stage_rows(pieces, flat, chan, rows):
    shards, per = pieces[0].shape[0], pieces[0].shape[1]
    for s in range(shards):
        for p, piece in enumerate(pieces):
            for i in range(per):
                a = (s * len(pieces) + p) * per + i
                flat[pl.ds(a, chan, stride=rows), :] = piece[s, i].astype(F32)


def spectrum(flat, first, group, rows, kept, outer, tcos, tsin, ahead, work):
    wide = jnp.concatenate(
        [flat[pl.ds(pl.multiple_of((first + c) * rows, rows), rows), :] for c in range(group)], axis=1
    ).astype(BF16)
    mixed = dot(outer[...], jnp.concatenate([wide, wide], axis=0))
    for c in range(group):
        lanes = slice(c * LANES, (c + 1) * LANES)
        real, imag = mixed[:kept, lanes], mixed[kept:, lanes]
        work[c * kept : (c + 1) * kept, :LANES] = real * tcos[...] + imag * tsin[...]
        work[c * kept : (c + 1) * kept, LANES:] = imag * tcos[...] - real * tsin[...]
    return dot3(work[...], ahead)


def filter_kernel(group, filt, outer, tcos, tsin, ahead, out, flat, work):
    chan = filt.shape[2]
    rows = filt.shape[0] * filt.shape[1]
    kept = tcos.shape[0]
    stage_rows([filt], flat, chan, rows)

    def step(it, carry):
        first = it * group
        out[pl.ds(pl.multiple_of(first * kept, group * kept), group * kept), :] = spectrum(
            flat, first, group, rows, kept, outer, tcos, tsin, ahead, work
        )
        return carry

    lax.fori_loop(0, chan // group, step, 0)


def conv_kernel(group, part_a, part_b, spec, outer, tcos, tsin, ahead, back, closing, out, flat, work, flat_out):
    chan = part_a.shape[2]
    rows = 2 * part_a.shape[0] * part_a.shape[1]
    kept = tcos.shape[0]
    stage_rows([part_a, part_b], flat, chan, rows)

    def step(it, carry):
        first = it * group
        d = spectrum(flat, first, group, rows, kept, outer, tcos, tsin, ahead, work)
        h = spec[pl.ds(pl.multiple_of(first * kept, group * kept), group * kept), :]
        dr, di, hr, hi = d[:, :LANES], d[:, LANES:], h[:, :LANES], h[:, LANES:]
        work[:, :LANES] = dr * hr - di * hi
        work[:, LANES:] = dr * hi + di * hr
        e = dot3(work[...], back)
        reals, imags = [], []
        for c in range(group):
            er, ei = e[c * kept : (c + 1) * kept, :LANES], e[c * kept : (c + 1) * kept, LANES:]
            reals.append(er * tcos[...] - ei * tsin[...])
            imags.append(er * tsin[...] + ei * tcos[...])
        g = jnp.concatenate([jnp.concatenate(reals, 1), jnp.concatenate(imags, 1)], 0)
        high = g.astype(BF16)
        low = (g - high.astype(F32)).astype(BF16)
        y = dot(closing[...], jnp.concatenate([high, high, low], axis=0))
        for c in range(group):
            flat_out[pl.ds(first + c, rows, stride=chan), :] = y[:, c * LANES : (c + 1) * LANES]
        return carry

    lax.fori_loop(0, chan // group, step, 0)
    shards, per = out.shape[0], out.shape[1]
    for s in range(shards):
        for i in range(per):
            a = s * per + i
            out[s, i] = flat_out[a * chan : (a + 1) * chan, :].astype(BF16)


def vmem_params(**kw):
    return pltpu.CompilerParams(vmem_limit_bytes=48 * 1024 * 1024, **kw)


def filter_spectrum(filt, tb):
    shards, per, chan, _ = filt.shape
    rows, kept = tb["rows"], tb["kept"]
    group = math.gcd(chan, 8)
    return pl.pallas_call(
        functools.partial(filter_kernel, group),
        out_shape=jax.ShapeDtypeStruct((chan * kept, 2 * LANES), F32),
        in_specs=[pl.BlockSpec(memory_space=pltpu.VMEM)] * 5,
        out_specs=pl.BlockSpec(memory_space=pltpu.VMEM),
        scratch_shapes=[pltpu.VMEM((chan * rows, LANES), F32), pltpu.VMEM((group * kept, 2 * LANES), F32)],
        compiler_params=vmem_params(),
        cost_estimate=pl.CostEstimate(flops=2_000_000_000, bytes_accessed=4_000_000, transcendentals=0),
        name="filter_spectrum",
    )(filt, tb["outer"], tb["twist_cos"], tb["twist_sin"], tb["ahead"])


def long_conv(part_a, part_b, spec, tb):
    shards, per, chan, _ = part_a.shape
    rows, kept = tb["rows"], tb["kept"]
    group = math.gcd(chan, 8)
    return pl.pallas_call(
        functools.partial(conv_kernel, group),
        out_shape=jax.ShapeDtypeStruct((shards, 2 * per, chan, LANES), BF16),
        in_specs=[pl.BlockSpec(memory_space=pltpu.VMEM)] * 9,
        out_specs=pl.BlockSpec(memory_space=pltpu.VMEM),
        scratch_shapes=[
            pltpu.VMEM((chan * rows, LANES), F32),
            pltpu.VMEM((group * kept, 2 * LANES), F32),
            pltpu.VMEM((rows * chan, LANES), F32),
        ],
        compiler_params=vmem_params(),
        cost_estimate=pl.CostEstimate(flops=5_000_000_000, bytes_accessed=4_000_000, transcendentals=0),
        name="long_conv",
    )(part_a, part_b, spec, tb["outer"], tb["twist_cos"], tb["twist_sin"], tb["ahead"], tb["back"], tb["closing"])


def proj_kernel(n_blocks, chunks, head_rows, skip, last, *refs):
    refs = list(refs)
    refs.pop(0)
    head = refs.pop(0) if head_rows else None
    blocks = [refs.pop(0) for _ in range(n_blocks)]
    weight = refs.pop(0)
    before = refs.pop(0) if last else None
    tail = refs.pop(0) if last == "a" else None
    taps = refs.pop(0) if last else None
    acc = refs[-1] if not last else refs[-2]
    ch = weight.shape[2]
    step = pl.program_id(0)

    def add(block, first):
        rows = block[...]
        if skip:
            rows = rows[skip:]
        if head_rows:
            rows = jnp.concatenate([head[...], rows], axis=0)
        for s in range(3):
            lanes = slice(s * ch, (s + 1) * ch)
            term = dot(rows, weight[s])
            if first:
                acc[:, lanes] = term
            else:
                acc[:, lanes] += term

    @pl.when(step == 0)
    def _():
        if last:
            acc[...] = before[...]
            add(blocks[0], False)
        else:
            add(blocks[0], True)

    for j, block in enumerate(blocks):
        low, high = max(1, j * chunks), (j + 1) * chunks
        if low < high:

            @pl.when((step >= low) & (step < high))
            def _(block=block):
                add(block, False)

    if not last:
        return
    wide = refs[-1]
    outs = refs[:-2]

    @pl.when(step == n_blocks * chunks - 1)
    def _():
        query, product, turned = outs[:3]
        count = query.shape[0]
        rounded = acc[...].astype(BF16)
        if last == "b":
            outs[3][...] = rounded[:HALO]
            wide[...] = rounded.astype(F32)
        else:
            wide[: rounded.shape[0]] = rounded.astype(F32)
            wide[rounded.shape[0] :] = tail[...].astype(F32)
        for i in range(count // LANES):
            low = HALO + i * LANES

            def stream(s):
                lanes = slice(s * ch, (s + 1) * ch)
                return (
                    taps[0:1, lanes] * wide[low : low + LANES, lanes]
                    + taps[1:2, lanes] * wide[low - 1 : low - 1 + LANES, lanes]
                    + taps[2:3, lanes] * wide[low - 2 : low - 2 + LANES, lanes]
                )

            place = slice(i * LANES, (i + 1) * LANES)
            query[place] = stream(0)
            kv = stream(1) * stream(2)
            product[place] = kv.astype(BF16)
            flipped = kv.T
            shards, chan = turned.shape[0], turned.shape[2]
            for d in range(shards):
                turned[d, i] = flipped[d * chan : (d + 1) * chan].astype(BF16)


def project(order, blocks, weight, head=None, skip=0, before=None, tail=None, taps=None, last="", shards=1):
    n_blocks = len(blocks)
    depth = blocks[0].shape[1]
    chunk = min(512, depth)
    chunks = depth // chunk
    ch = weight.shape[2]
    head_rows = 0 if head is None else head.shape[0]
    height = blocks[0].shape[0] - skip + head_rows
    steps = n_blocks * chunks
    in_specs, args = [], []
    if head is not None:
        in_specs.append(pl.BlockSpec((head_rows, chunk), lambda i, o: (0, i)))
        args.append(head)
    for j, block in enumerate(blocks):
        in_specs.append(
            pl.BlockSpec(
                (block.shape[0], chunk), lambda i, o, j=j: (0, jnp.clip(i - j * chunks, 0, chunks - 1))
            )
        )
        args.append(block)
    in_specs.append(pl.BlockSpec((3, chunk, ch), lambda i, o: (0, o[i], 0)))
    args.append(weight)

    def whole(shape):
        return pl.BlockSpec(shape, lambda i, o: (0,) * len(shape), pipeline_mode=pl.Buffered(1))

    if last:
        in_specs.append(whole(before.shape))
        args.append(before)
        if tail is not None:
            in_specs.append(whole(tail.shape))
            args.append(tail)
        in_specs.append(whole(taps.shape))
        args.append(taps)
    scratch = []
    if last:
        count = height if last == "a" else height - HALO
        shapes = [
            jax.ShapeDtypeStruct((count, ch), F32),
            jax.ShapeDtypeStruct((count, ch), BF16),
            jax.ShapeDtypeStruct((shards, count // LANES, ch // shards, LANES), BF16),
        ]
        if last == "b":
            shapes.append(jax.ShapeDtypeStruct((HALO, 3 * ch), BF16))
        scratch = [pltpu.VMEM((height, 3 * ch), F32), pltpu.VMEM((count + HALO, 3 * ch), F32)]
    else:
        shapes = [jax.ShapeDtypeStruct((height, 3 * ch), F32)]
    return pl.pallas_call(
        functools.partial(proj_kernel, n_blocks, chunks, head_rows, skip, last),
        out_shape=shapes,
        grid_spec=pltpu.PrefetchScalarGridSpec(
            num_scalar_prefetch=1,
            grid=(steps,),
            in_specs=in_specs,
            out_specs=[
                pl.BlockSpec(s.shape, lambda i, o, n=len(s.shape): (0,) * n, pipeline_mode=pl.Buffered(1))
                for s in shapes
            ],
            scratch_shapes=scratch,
        ),
        compiler_params=vmem_params(dimension_semantics=("arbitrary",)),
        cost_estimate=pl.CostEstimate(
            flops=2 * height * steps * chunk * 3 * ch, bytes_accessed=steps * chunk * 3 * ch * 2, transcendentals=0
        ),
        name="project_" + (last or "part"),
    )(order, *args)


def gate_kernel(query, product, back, skip, out):
    groups, per, chan, _ = back.shape
    for i in range(per):
        place = slice(i * LANES, (i + 1) * LANES)
        conv = jnp.concatenate([back[g, i].astype(F32) for g in range(groups)], axis=0).T
        out[place] = (query[place] * (conv + skip[...] * product[place].astype(F32))).astype(BF16)


def gate(query, product, back, skip):
    count, ch = query.shape
    return pl.pallas_call(
        gate_kernel,
        out_shape=jax.ShapeDtypeStruct((count, ch), BF16),
        in_specs=[pl.BlockSpec(memory_space=pltpu.VMEM)] * 4,
        out_specs=pl.BlockSpec(memory_space=pltpu.VMEM),
        compiler_params=vmem_params(),
        cost_estimate=pl.CostEstimate(flops=4_000_000, bytes_accessed=3_000_000, transcendentals=0),
        name="gate",
    )(query, product, back, skip)


def mix_kernel(n_blocks, has_before, *refs):
    rows, weights = refs[:n_blocks], refs[n_blocks : 2 * n_blocks]
    out = refs[-1]
    total = refs[2 * n_blocks][...] if has_before else None
    for row, weight in zip(rows, weights):
        term = dot(row[...], weight[...])
        total = term if total is None else total + term
    out[...] = total.astype(out.dtype)


def mix(rows, weights, before=None):
    height, depth = rows[0].shape
    width = weights[0].shape[1]
    tile = min(256, width)
    n = len(rows)
    specs = [pl.BlockSpec((height, depth), lambda i: (0, 0))] * n
    specs += [pl.BlockSpec((depth, tile), lambda i: (0, i))] * n
    args = list(rows) + list(weights)
    if before is not None:
        specs.append(pl.BlockSpec((height, tile), lambda i: (0, i)))
        args.append(before)
    return pl.pallas_call(
        functools.partial(mix_kernel, n, before is not None),
        out_shape=jax.ShapeDtypeStruct((height, width), F32 if before is None else BF16),
        grid=(width // tile,),
        in_specs=specs,
        out_specs=pl.BlockSpec((height, tile), lambda i: (0, i)),
        compiler_params=vmem_params(dimension_semantics=("arbitrary",)),
        cost_estimate=pl.CostEstimate(
            flops=2 * n * height * depth * width, bytes_accessed=2 * n * depth * (height + width), transcendentals=0
        ),
        name="mix_last" if before is not None else "mix_part",
    )(*args)


def swap(value, mask):
    count = lax.axis_size("tp")
    return lax.ppermute(value, "tp", [(i, i ^ mask) for i in range(count)])


def spread(block, bits):
    held = {0: block}
    for bit in bits:
        held.update({mask ^ bit: swap(value, bit) for mask, value in list(held.items())})
    return held


def local(tokens, w_in, conv_taps, long_filter, skip_gain, w_out):
    n_tp, n_ctx = lax.axis_size("tp"), lax.axis_size("ctx")
    me = lax.axis_index("tp")
    count, depth = tokens.shape
    ch = w_in.shape[2]
    per = count // LANES
    chan = ch // n_ctx
    tb = tables(count * n_ctx)
    weight = w_in.transpose(1, 0, 2)
    taps = conv_taps.reshape(3, 3 * ch)
    far = n_tp // 2
    bits = []
    bit = far // 2
    while bit:
        bits.append(bit)
        bit //= 2
    cut = count // 2 - HALO

    far_b = swap(tokens[cut:], far)
    far_a = swap(tokens[:cut], far)
    near = spread(tokens, bits)
    masks = list(near)
    far_b = spread(far_b, bits)
    far_a = spread(far_a, bits)

    chunk = min(512, depth)
    chunks = depth // chunk

    def order(far_bit):
        owners = jnp.stack([me ^ (m ^ far_bit) for m in masks]).astype(jnp.int32)
        return (owners[:, None] * chunks + jnp.arange(chunks, dtype=jnp.int32)[None, :]).reshape(-1)

    filt = lax.all_to_all(
        long_filter.reshape(per, LANES, n_ctx, chan).transpose(2, 0, 3, 1), "ctx", 0, 0, tiled=True
    )
    spec = filter_spectrum(filt, tb)

    (acc_b,) = project(order(0), [near[m] for m in masks], weight, skip=cut)
    query_b, product_b, turned_b, middle = project(
        order(far), [far_b[m] for m in masks], weight, before=acc_b, taps=taps, last="b", shards=n_ctx
    )
    ends = jnp.concatenate(
        [near[m][count - HALO :] for m in masks] + [far_b[m][-HALO:] for m in masks], axis=1
    )
    ends = lax.ppermute(ends, "ctx", [(i, i + 1) for i in range(n_ctx - 1)])
    half = len(masks) * depth
    (acc_a,) = project(order(0), [near[m][:cut] for m in masks], weight, head=ends[:, :half])
    query_a, product_a, turned_a = project(
        order(far), [far_a[m] for m in masks], weight, head=ends[:, half:], before=acc_a, tail=middle,
        taps=taps, last="a", shards=n_ctx,
    )
    part_b = lax.all_to_all(turned_b, "ctx", 0, 0, tiled=True)
    part_a = lax.all_to_all(turned_a, "ctx", 0, 0, tiled=True)
    conv = long_conv(part_a, part_b, spec, tb)
    back = lax.all_to_all(conv, "ctx", 0, 0, tiled=True)
    query = jnp.concatenate([query_a, query_b], axis=0)
    product = jnp.concatenate([product_a, product_b], axis=0)
    gated = gate(query, product, back, skip_gain[None, :])

    width = w_out.shape[1] // n_tp
    far_g = spread(swap(gated, far), bits)
    near_g = spread(gated, bits)
    tied, _ = lax.optimization_barrier((w_out, middle))
    pieces = {}
    for m in range(n_tp):
        source = w_out if m < far else tied
        block = lax.dynamic_slice(source, (0, (me ^ m) * width), (ch, width))
        pieces[m] = swap(block, m) if m else block
    part = mix([near_g[m] for m in masks], [pieces[m] for m in masks])
    return mix([far_g[m] for m in masks], [pieces[m ^ far] for m in masks], before=part)


def solution(mesh):
    in_specs = (
        P("ctx", "tp"),
        P(None, None, "tp"),
        P(None, None, "tp"),
        P("ctx", "tp"),
        P("tp"),
        P("tp", None),
    )
    return jax.shard_map(local, mesh=mesh, in_specs=in_specs, out_specs=P("ctx", "tp"), check_vma=False)
```
